512 devices in a mesh: view: 16 (over z, core), tm: 32 (over y, x).
Axes of the slice: x: 4, y: 8, z: 8, core: 2. Of those that a mesh axis runs over, the one named last changes fastest.
Arguments:
- frames: bfloat16 [16, 128, 160, 640], P('view', 'tm'), may hold values from -6 to 6
- ln_gain: float32 [640], replicated, may hold values from 0.1 to 1.9
- w_query: bfloat16 [640, 640], replicated, as said below
- w_key: bfloat16 [640, 640], replicated, as said below
- w_value: bfloat16 [640, 640], replicated, may hold values from -0.25 to 0.25
- w_out: bfloat16 [640, 640], replicated, may hold values from -1 to 1
- conv_gain: float32 [640], replicated, may hold values from 0.1 to 1.9
- conv_weight: bfloat16 [1920, 640], P('tm'), may hold values from -0.25 to 0.25
Outputs:
- block_out: bfloat16 [16, 128, 160, 640], P('view', 'tm')
The draws below stay inside these ranges and needn't reach their ends.
Inputs may be any that keep to these rules, and one draw needn't show every extreme that they name: `w_query`: a projection matrix. `w_key`: a projection matrix.
All inputs are finite; a program needn't handle non-finite values.
Results may differ from the reference program's by a relative error of at most 0.006.
The reference program's roundings to bfloat16 on the way (of `normed`, `weights`, `attended`, `hidden` and `activated`) count: a program that leaves them out, or rounds other values in their place, can miss the bound.
Values may be sent and summed in bfloat16 or wider, within the bound.
No kernel may reach another device: no remote copies, remote signals or barrier semaphores. Data moves between devices by JAX's collectives and lax.ppermute only.
A program may use at most 64 MiB of HBM per device.

```python
import jax
import jax.numpy as jnp
from jax import lax

HEADS = 10
HEAD_DIM = 64
C = 640
TOK = 160
VIEWS = 16
FRAMES = 128


def shared_projections(key):
    base = jax.random.normal(jax.random.fold_in(key, 11), (C, C), jnp.float32)
    noise = jax.random.normal(jax.random.fold_in(key, 12), (C, C), jnp.float32)
    scale = C ** (-0.5)
    first = 2.0 * scale * base
    second = 2.0 * scale * noise
    return (first, second)


def draw_w_query(key, part):
    first, second = shared_projections(key)
    return first.astype(jnp.bfloat16)


def draw_w_key(key, part):
    first, second = shared_projections(key)
    return second.astype(jnp.bfloat16)


def shard_levels(key, extent, split, least, high):
    level = 1.0
    for axis_at, shards_of in split:
        draws = jax.random.uniform(jax.random.fold_in(jax.random.fold_in(key, 6), axis_at), (shards_of,), jnp.float32, least / len(split), high / len(split))
        level = level * jnp.repeat(jnp.exp(draws), extent[axis_at] // shards_of).reshape((-1,) + (1,) * (len(extent) - 1 - axis_at))
    return level


def bell_draw(key, shape, deviation, most, cuts=(), dtype=jnp.bfloat16):
    loudness = shard_levels(key, shape, cuts, -0.22, 0.18) if cuts else 1.0
    array = jax.random.normal(key, shape, jnp.float32) * deviation * loudness
    return jnp.minimum(jnp.maximum(array, -most), most).astype(dtype)


def setup_inputs(seed: int = 0) -> dict:
    seeds = jax.random.split(jax.random.key(seed), 9)
    return {
        "frames": bell_draw(seeds[0], (VIEWS, FRAMES, TOK, C), 1.0, 6.0, ((0, 16), (1, 32))),
        "ln_gain": jnp.clip(1.0 + 0.18 * jax.random.normal(seeds[1], (C,), jnp.float32), 0.1, 1.9),
        "w_query": draw_w_query(jax.random.fold_in(seeds[8], 71), 0),
        "w_key": draw_w_key(jax.random.fold_in(seeds[8], 71), 0),
        "w_value": bell_draw(seeds[4], (C, C), C ** -0.5, 0.25),
        "w_out": bell_draw(seeds[5], (C, C), (C // 16) ** -0.5, 1.0),
        "conv_gain": jnp.clip(1.0 + 0.18 * jax.random.normal(seeds[6], (C,), jnp.float32), 0.1, 1.9),
        "conv_weight": bell_draw(seeds[7], (3 * C, C), C ** -0.5, 0.25, ((0, 32),)),
    }


def layer_norm(values, gain):
    mean = lax.optimization_barrier(jnp.mean(values, axis=-1, keepdims=True))
    centred = values - mean
    variance = lax.optimization_barrier(jnp.mean(centred * centred, axis=-1, keepdims=True))
    return centred * lax.rsqrt(variance + 1e-05) * gain

def attend(query, keyset, valueset):
    rows = query.shape[0]
    heads_q = query.reshape(rows, HEADS, HEAD_DIM).transpose(1, 0, 2)
    heads_k = keyset.reshape(keyset.shape[0], HEADS, HEAD_DIM).transpose(1, 0, 2)
    heads_v = valueset.reshape(valueset.shape[0], HEADS, HEAD_DIM).transpose(1, 0, 2)

    def one_head(trio):
        head_q, head_k, head_v = trio
        scores = jnp.dot(head_q, head_k.T, preferred_element_type=jnp.float32) * HEAD_DIM ** (-0.5)
        top = lax.optimization_barrier(jnp.max(scores, axis=-1, keepdims=True))
        expo = jnp.exp(scores - top)
        weights = (expo / lax.optimization_barrier(jnp.sum(expo, axis=-1, keepdims=True))).astype(jnp.bfloat16)
        return jnp.dot(weights, head_v, preferred_element_type=jnp.float32)
    outputs = lax.map(one_head, (heads_q, heads_k, heads_v))
    return outputs.transpose(1, 0, 2).reshape(rows, HEADS * HEAD_DIM).astype(jnp.bfloat16)

def reference(frames, ln_gain, w_query, w_key, w_value, w_out, conv_gain, conv_weight):
    tokens = frames.astype(jnp.float32)
    normed = layer_norm(tokens, ln_gain).astype(jnp.bfloat16)
    flat = normed.reshape(-1, C)
    query = jnp.dot(flat, w_query, preferred_element_type=jnp.float32).astype(jnp.bfloat16).reshape(normed.shape)
    keys = jnp.dot(flat, w_key, preferred_element_type=jnp.float32).astype(jnp.bfloat16).reshape(normed.shape)
    values = jnp.dot(flat, w_value, preferred_element_type=jnp.float32).astype(jnp.bfloat16).reshape(normed.shape)
    prev_keys = jnp.concatenate([keys[:, :1], keys[:, :-1]], axis=1)
    prev_values = jnp.concatenate([values[:, :1], values[:, :-1]], axis=1)
    anchor_keys = keys[0, 0]
    anchor_values = values[0, 0]

    def one_frame(trio):
        frame_q, frame_k, frame_v = trio
        keyset = jnp.concatenate([anchor_keys, frame_k], axis=0)
        valueset = jnp.concatenate([anchor_values, frame_v], axis=0)
        return attend(frame_q, keyset, valueset)
    attended = lax.map(one_frame, (query.reshape(-1, TOK, C), prev_keys.reshape(-1, TOK, C), prev_values.reshape(-1, TOK, C)))
    mixed = jnp.dot(attended.reshape(-1, C), w_out, preferred_element_type=jnp.float32).reshape(tokens.shape)
    hidden = (tokens + mixed).astype(jnp.bfloat16)
    activated = jax.nn.silu(layer_norm(hidden.astype(jnp.float32), conv_gain)).astype(jnp.bfloat16)
    zeros = jnp.zeros_like(activated[:, :1])
    before = jnp.concatenate([zeros, activated[:, :-1]], axis=1)
    after = jnp.concatenate([activated[:, 1:], zeros], axis=1)
    stacked = jnp.concatenate([before, activated, after], axis=-1).reshape(-1, 3 * C)
    conv = jnp.dot(stacked, conv_weight, preferred_element_type=jnp.float32).reshape(tokens.shape)
    return (hidden.astype(jnp.float32) + conv).astype(jnp.bfloat16)
```

```python
import jax
import jax.numpy as jnp
from jax import lax
from jax.experimental import pallas as pl
from jax.experimental.pallas import tpu as pltpu
from jax.sharding import PartitionSpec as P

HEADS = 10
HEAD_DIM = 64
PAIR = 2 * HEAD_DIM
C = 640
TOK = 160
X, Y, Z = 4, 8, 8
TM = X * Y
AXES = ("view", "tm")
VMEM = pl.BlockSpec(memory_space=pltpu.VMEM)
SMEM = pl.BlockSpec(memory_space=pltpu.SMEM)


def device(y, x, z, core):
    return (z * 2 + core) * TM + y * X + x


def all_devices():
    return [
        (y, x, z, c) for z in range(Z) for c in range(2) for y in range(Y) for x in range(X)
    ]


def layer_norm(values, gain):
    mean = jnp.mean(values, axis=-1, keepdims=True)
    centred = values - mean
    variance = jnp.mean(centred * centred, axis=-1, keepdims=True)
    return centred * lax.rsqrt(variance + 1e-05) * gain


def matmul(a, b):
    return jnp.dot(a, b, preferred_element_type=jnp.float32)


def tree_rounds():
    steps = [(0, 4), (0, 2), (0, 1), (1, 2), (1, 1), (2, 4), (2, 2), (2, 1), (3, 1)]
    holders = [(0, 0, 0, 0)]
    for dim, distance in steps:
        fresh = []
        for place in holders:
            target = list(place)
            target[dim] += distance
            fresh.append((place, tuple(target)))
        holders = holders + [target for _, target in fresh]
        yield dim, distance, [(device(*a), device(*b)) for a, b in fresh]


def spread_anchor(frame, place):
    held = frame
    for dim, distance, pairs in tree_rounds():
        got = lax.ppermute(held, AXES, pairs)
        mine = place[dim] % (2 * distance) == distance
        for later in range(dim + 1, 4):
            mine = mine & (place[later] == 0)
        held = jnp.where(mine, got, held)
    return held


def gather_conv(shard):
    places = all_devices()
    near = lax.ppermute(
        shard, AXES, [(device(y, x ^ 1, z, c), device(y, x, z, c)) for y, x, z, c in places]
    )
    two = jnp.stack([shard, near])
    far = lax.ppermute(
        two, AXES, [(device(y, x ^ 2, z, c), device(y, x, z, c)) for y, x, z, c in places]
    )
    own = jnp.concatenate([two, far])
    ring = [
        (device((y + (2 * c - 1)) % Y, x, z, c), device(y, x, z, c)) for y, x, z, c in places
    ]
    blocks, held = [], own
    for _ in range(4):
        held = lax.ppermute(held, AXES, ring)
        blocks.append(held)
    mine = jnp.stack([blocks[0], blocks[1], blocks[2], blocks[3]])
    partner = lax.ppermute(
        mine, AXES, [(device(y, x, z, 1 - c), device(y, x, z, c)) for y, x, z, c in places]
    )
    return own, mine, partner


def project_kernel(tok, gain, w_q, w_k, w_v, q, k, v):
    def frame(f, carry):
        rows = pl.ds(pl.multiple_of(f * TOK, TOK), TOK)
        normed = layer_norm(tok[rows, :].astype(jnp.float32), gain[...]).astype(jnp.bfloat16)
        q[rows, :] = (
            matmul(normed, w_q[...]).astype(jnp.bfloat16).astype(jnp.float32) * HEAD_DIM**-0.5
        ).astype(jnp.bfloat16)
        k[rows, :] = matmul(normed, w_k[...]).astype(jnp.bfloat16)
        v[rows, :] = matmul(normed, w_v[...]).astype(jnp.bfloat16)
        return carry

    lax.fori_loop(0, tok.shape[0] // TOK, frame, 0)


def attend_kernel(
    where, tok, q, k, v, anchor, before, gain, w_k, w_v, w_out, conv_gain,
    hidden, active, keys, values, attended,
):
    first = where[0] == 0
    edge = jnp.where(first, tok[:TOK, :], before[...])
    both = jnp.concatenate([anchor[...], edge], axis=0).astype(jnp.float32)
    normed = layer_norm(both, gain[...]).astype(jnp.bfloat16)
    keys[...] = matmul(normed, w_k[...]).astype(jnp.bfloat16)
    values[...] = matmul(normed, w_v[...]).astype(jnp.bfloat16)

    def frame(f, carry):
        rows = pl.ds(pl.multiple_of(f * TOK, TOK), TOK)
        low = lax.broadcasted_iota(jnp.int32, (TOK, PAIR), 1) < HEAD_DIM
        for pair in range(HEADS // 2):
            lanes = slice(pair * PAIR, (pair + 1) * PAIR)
            query = q[rows, lanes]
            none = jnp.zeros_like(query)
            keyset, valueset = keys[:, lanes], values[:, lanes]
            outs = []
            for chosen in (low, jnp.logical_not(low)):
                scores = lax.dot_general(
                    jnp.where(chosen, query, none), keyset,
                    (((1,), (1,)), ((), ())), preferred_element_type=jnp.float32,
                )
                top = jnp.max(scores, axis=-1, keepdims=True)
                expo = jnp.exp(scores - top)
                total = jnp.sum(expo, axis=-1, keepdims=True)
                weights = (expo * (1.0 / total)).astype(jnp.bfloat16)
                outs.append(matmul(weights, valueset))
            attended[:, lanes] = jnp.where(low, outs[0], outs[1]).astype(jnp.bfloat16)
        mixed = matmul(attended[...], w_out[...])
        hid = (tok[rows, :].astype(jnp.float32) + mixed).astype(jnp.bfloat16)
        hidden[rows, :] = hid
        scaled = layer_norm(hid.astype(jnp.float32), conv_gain[...])
        active[rows, :] = (scaled * (1.0 / (1.0 + jnp.exp(-scaled)))).astype(jnp.bfloat16)
        keys[TOK:, :] = k[rows, :]
        values[TOK:, :] = v[rows, :]
        return carry

    lax.fori_loop(0, tok.shape[0] // TOK, frame, 0)


def conv_kernel(where, hidden, active, before, after, own, mine, partner, out, weight):
    x, y, sign = where[1], where[2], 1 - 2 * where[3]

    def place(source, row):
        block = jnp.concatenate([source[i ^ x] for i in range(X)], axis=0)
        weight[pl.ds(pl.multiple_of(row * 240, 16), 240), :] = block

    place(own, y)
    for s in range(4):
        place(mine.at[s], (y - sign * (s + 1)) & (Y - 1))
        place(partner.at[s], (y + sign * (s + 1)) & (Y - 1))
    count = hidden.shape[0] // TOK
    for f in range(count):
        rows = slice(f * TOK, (f + 1) * TOK)
        prior = before[...] if f == 0 else active[(f - 1) * TOK : f * TOK, :]
        later = after[...] if f == count - 1 else active[(f + 1) * TOK : (f + 2) * TOK, :]
        total = matmul(prior, weight[:C, :])
        total += matmul(active[rows, :], weight[C : 2 * C, :])
        total += matmul(later, weight[2 * C :, :])
        out[rows, :] = (hidden[rows, :].astype(jnp.float32) + total).astype(jnp.bfloat16)


def call(kernel, name, specs, outs, scratch, flops, *operands):
    moved = sum(a.size * a.dtype.itemsize for a in operands)
    return pl.pallas_call(
        kernel,
        name=name,
        out_shape=[jax.ShapeDtypeStruct(s, jnp.bfloat16) for s in outs],
        in_specs=specs,
        out_specs=[VMEM] * len(outs),
        scratch_shapes=scratch,
        compiler_params=pltpu.CompilerParams(vmem_limit_bytes=48 << 20),
        cost_estimate=pl.CostEstimate(flops=flops, bytes_accessed=moved, transcendentals=0),
    )(*operands)


def per_device(frames, ln_gain, w_query, w_key, w_value, w_out, conv_gain, conv_weight):
    local = frames.shape[1]
    tok = frames[0].reshape(local * TOK, C)
    view, tm = lax.axis_index("view"), lax.axis_index("tm")
    x, y, z, core = tm % X, tm // X, view // 2, view % 2
    where = jnp.stack([tm, x, y, core]).astype(jnp.int32)
    gain, gain2 = ln_gain.reshape(1, C), conv_gain.reshape(1, C)
    rows = local * TOK
    onward = [(i, i + 1) for i in range(TM - 1)]
    backward = [(i + 1, i) for i in range(TM - 1)]

    anchor = spread_anchor(tok[:TOK], (y, x, z, core))
    before = lax.ppermute(tok[-TOK:], "tm", onward)
    own, mine, partner = gather_conv(conv_weight)
    q, k, v = call(
        project_kernel, "project", [VMEM] * 5, [(rows, C)] * 3, [], 6 * rows * C * C,
        tok, gain, w_query, w_key, w_value,
    )
    hidden, active = call(
        attend_kernel, "attend", [SMEM] + [VMEM] * 11, [(rows, C)] * 2,
        [pltpu.VMEM((2 * TOK, C), jnp.bfloat16), pltpu.VMEM((2 * TOK, C), jnp.bfloat16),
         pltpu.VMEM((TOK, C), jnp.bfloat16)],
        8 * rows * C * C,
        where, tok, q, k, v, anchor, before, gain, w_key, w_value, w_out, gain2,
    )
    prior = lax.ppermute(active[-TOK:], "tm", onward)
    later = lax.ppermute(active[:TOK], "tm", backward)
    (out,) = call(
        conv_kernel, "conv", [SMEM] + [VMEM] * 7, [(rows, C)],
        [pltpu.VMEM((3 * C, C), jnp.bfloat16)], 6 * rows * C * C,
        where, hidden, active, prior, later, own, mine, partner,
    )
    return out.reshape(1, local, TOK, C)


def solution(mesh):
    placed = (P("view", "tm", None, None), P(), P(), P(), P(), P(), P(), P("tm", None))
    return jax.shard_map(
        per_device,
        mesh=mesh,
        in_specs=placed,
        out_specs=P("view", "tm", None, None),
        check_vma=False,
    )
```

```python
import jax
import jax.numpy as jnp
from jax import lax
from jax.experimental import pallas as pl
from jax.experimental.pallas import tpu as pltpu
from jax.sharding import PartitionSpec as P


HEADS = 10
HEAD_DIM = 64
PAIR = 2 * HEAD_DIM
C = 640
TOK = 160
X, Y, Z = 4, 8, 8
TM = X * Y
AXES = ("view", "tm")
VMEM = pl.BlockSpec(memory_space=pltpu.VMEM)
SMEM = pl.BlockSpec(memory_space=pltpu.SMEM)
HBM = pl.BlockSpec(memory_space=pltpu.HBM)
ANY = pl.BlockSpec(memory_space=pl.ANY)
SHARD = 60
SLOT = 64
LIMIT_BYTES = 67043328


def device(y, x, z, core):
    return (z * 2 + core) * TM + y * X + x


def all_devices():
    return [
        (y, x, z, c) for z in range(Z) for c in range(2) for y in range(Y) for x in range(X)
    ]


def layer_norm(values, gain):
    mean = jnp.mean(values, axis=-1, keepdims=True)
    centred = values - mean
    variance = jnp.mean(centred * centred, axis=-1, keepdims=True)
    return centred * lax.rsqrt(variance + 1e-05) * gain


def matmul(a, b):
    return jnp.dot(a, b, preferred_element_type=jnp.float32)


ORDERS = (
    ((0, 4), (0, 2), (0, 1), (1, 2), (1, 1), (2, 4), (2, 2), (2, 1)),
    ((2, 4), (2, 2), (2, 1), (1, 2), (1, 1), (0, 4), (0, 2), (0, 1)),
)


def tree_pairs():
    holders = [[(0, 0, 0)], [(0, 0, 0)]]
    for step in range(8):
        pairs = []
        for core in range(2):
            dim, distance = ORDERS[core][step]
            fresh = []
            for place in holders[core]:
                target = list(place)
                target[dim] += distance
                fresh.append(tuple(target))
                pairs.append((device(*place, core), device(*target, core)))
            holders[core] = holders[core] + fresh
        yield pairs


def receives(step, place, core):
    flags = []
    for order in ORDERS:
        dim, distance = order[step]
        flag = place[dim] % (2 * distance) == distance
        seen = [d for d, _ in order[: step + 1]]
        for later in range(3):
            if later not in seen:
                flag = flag & (place[later] == 0)
        flags.append(flag)
    return jnp.where(core == 0, flags[0], flags[1])


def swapped_cores():
    return [(device(y, x, z, 1 - c), device(y, x, z, c)) for y, x, z, c in all_devices()]


def transfers(tok, last, first, shard, place, core):
    places = all_devices()
    half = TOK // 2
    second = tok[half:TOK]
    got = lax.ppermute(second, AXES, [(device(0, 0, 0, 0), device(0, 0, 0, 1))])
    top = lax.optimization_barrier(tok[:half])
    held = lax.select(jnp.broadcast_to(core == 0, got.shape), top, got)
    for step, pairs in enumerate(tree_pairs()):
        got = lax.ppermute(held, AXES, pairs)
        fresh = jnp.broadcast_to(receives(step, place, core), got.shape)
        held = lax.select(fresh, got, held)
    other = lax.ppermute(held, AXES, swapped_cores())
    behind = lax.ppermute(first, "tm", [(i + 1, i) for i in range(TM - 1)])
    before = lax.ppermute(last, "tm", [(i, i + 1) for i in range(TM - 1)])

    near = lax.ppermute(
        shard, AXES,
        [(device(y, x ^ 1, z, c), device(y, x, z, c)) for y, x, z, c in places],
    )
    slack = jnp.zeros((SLOT - SHARD, C), shard.dtype)
    two = jnp.concatenate([shard, slack, near, slack])
    far = lax.ppermute(
        two, AXES,
        [(device(y, x ^ 2, z, c), device(y, x, z, c)) for y, x, z, c in places],
    )
    own = jnp.concatenate([two, far])
    ring = [
        (device((y + (2 * c - 1)) % Y, x, z, c), device(y, x, z, c)) for y, x, z, c in places
    ]
    blocks = [own]
    for _ in range(4):
        blocks.append(lax.ppermute(blocks[-1], AXES, ring))
    partner = lax.ppermute(jnp.concatenate(blocks[1:4]), AXES, swapped_cores())
    return held, other, before, behind, blocks, partner


def transposed(values):
    return jnp.transpose(values.astype(jnp.float32)).astype(jnp.bfloat16)


def contract_lanes(a, b):
    return lax.dot_general(a, b, (((1,), (1,)), ((), ())), preferred_element_type=jnp.float32)


def swap_heads(a):
    return jnp.concatenate([a[:, HEAD_DIM:], a[:, :HEAD_DIM]], axis=1)


def fetch(pairs, sems):
    sems, start = sems if isinstance(sems, tuple) else (sems, 0)
    copies = [pltpu.make_async_copy(a, b, sems.at[start + i]) for i, (a, b) in enumerate(pairs)]
    for copy in copies:
        copy.start()
    return copies


def query_kernel(
    tok_hbm, w_hbm, gain, normed_hbm, q_hbm, last_hbm, first_hbm, tok, w, normed, q, sems,
    out_sems,
):
    copies = fetch(((tok_hbm, tok), (w_hbm, w)), sems)
    rows = tok.shape[0]
    copies[0].wait()
    stores = fetch(
        ((tok.at[rows - 2 * TOK :, :], last_hbm), (tok.at[:TOK, :], first_hbm)), out_sems
    )
    gains = gain[...].reshape(1, C)
    for at in range(0, rows, TOK):
        part = layer_norm(tok[at : at + TOK, :].astype(jnp.float32), gains)
        normed[at : at + TOK, :] = part.astype(jnp.bfloat16)
    stores += fetch(((normed, normed_hbm),), (out_sems, 2))
    copies[1].wait()
    q[...] = scaled_query(normed[...], w[...])
    stores += fetch(((q, q_hbm),), (out_sems, 3))
    for store in stores:
        store.wait()


def scaled_query(normed, w):
    part = matmul(normed, w).astype(jnp.bfloat16)
    return (part.astype(jnp.float32) * HEAD_DIM**-0.5).astype(jnp.bfloat16)


def keys_kernel(
    normed_hbm, w_k_hbm, w_v_hbm, k_hbm, v_hbm, normed, w_k, w_v, k, v, sems, out_sems
):
    copies = fetch(((normed_hbm, normed), (w_k_hbm, w_k), (w_v_hbm, w_v)), sems)
    copies[0].wait()
    copies[1].wait()
    k[...] = matmul(normed[...], w_k[...]).astype(jnp.bfloat16)
    stores = fetch(((k, k_hbm),), out_sems)
    copies[2].wait()
    for f in range(v.shape[0]):
        v[f] = transposed(matmul(normed[f * TOK : (f + 1) * TOK, :], w_v[...]))
    stores += fetch(((v, v_hbm),), (out_sems, 1))
    for store in stores:
        store.wait()


def block_kernel(
    gain, conv_gain, held, other, before, behind, w_k_hbm, w_v_hbm, w_q_hbm, q_hbm, k_hbm,
    v_hbm, tok_hbm, w_out_hbm, hidden_hbm, active_hbm,
    w_k, w_v, w_q, w_out, tok, q, keys, values, anchor_key, anchor_value, halves, earlier,
    attended, hidden, active, sems, out_sems,
):
    count = tok_hbm.shape[0] // TOK
    rows, wide = count * TOK, (count + 2) * TOK
    tm = lax.axis_index("tm")
    core = lax.rem(lax.axis_index("view"), 2)
    starts, ends = tm == 0, tm == TM - 1

    @pl.when(starts)
    def _():
        pltpu.make_async_copy(tok_hbm.at[:TOK, :], tok.at[:TOK, :], sems.at[0]).start()

    @pl.when(jnp.logical_not(starts))
    def _():
        pltpu.make_async_copy(before.at[TOK:, :], tok.at[:TOK, :], sems.at[0]).start()

    inputs = fetch(
        (
            (held, halves.at[core]), (other, halves.at[1 - core]),
            (before.at[:TOK, :], earlier), (behind, tok.at[rows + TOK :, :]),
        ),
        (sems, 1),
    )
    copies = fetch(
        (
            (w_k_hbm, w_k), (w_v_hbm, w_v), (w_q_hbm, w_q), (q_hbm, q.at[TOK : rows + TOK, :]),
            (k_hbm, keys.at[2 * TOK :, :]), (v_hbm, values.at[2:]),
            (w_out_hbm, w_out), (tok_hbm, tok.at[TOK : rows + TOK, :]),
        ),
        (sems, 5),
    )
    pltpu.make_async_copy(before.at[TOK:, :], tok.at[:TOK, :], sems.at[0]).wait()
    for copy in inputs:
        copy.wait()

    def norm(raw):
        part = layer_norm(raw.astype(jnp.float32), gain[...].reshape(1, C))
        return part.astype(jnp.bfloat16)

    anchor = norm(jnp.concatenate([halves[0], halves[1]], axis=0))
    second, first = norm(earlier[...]), norm(tok[:TOK, :])
    final = norm(tok[rows + TOK :, :])
    copies[0].wait()
    anchor_key[...] = matmul(anchor, w_k[...]).astype(jnp.bfloat16)
    keys[:TOK, :] = matmul(second, w_k[...]).astype(jnp.bfloat16)
    keys[TOK : 2 * TOK, :] = matmul(first, w_k[...]).astype(jnp.bfloat16)
    copies[1].wait()
    anchor_value[...] = transposed(matmul(anchor, w_v[...]))
    values[0] = transposed(matmul(second, w_v[...]))
    values[1] = transposed(matmul(first, w_v[...]))
    copies[2].wait()
    q[:TOK, :] = scaled_query(first, w_q[...])
    q[rows + TOK :, :] = scaled_query(final, w_q[...])
    for copy in copies[3:6]:
        copy.wait()

    part = wide // 2
    frame = lax.broadcasted_iota(jnp.int32, (1, part), 1)
    low = lax.broadcasted_iota(jnp.int32, (part, PAIR), 1) < HEAD_DIM
    for group in range(2):
        at_q = slice(group * part, (group + 1) * part)
        for pair in range(HEADS // 2):
            lanes = slice(pair * PAIR, (pair + 1) * PAIR)
            query = q[at_q, lanes]
            turned = swap_heads(query)
            none = jnp.zeros_like(query)
            fixed = anchor_key[:, lanes]
            prior = [
                keys[group * part + f * TOK : group * part + (f + 1) * TOK, lanes]
                for f in range(3)
            ]
            for head in range(2):
                at_low, at_high = (query, turned) if head == 0 else (turned, query)
                evens = jnp.where(low, at_low, none)
                odds = jnp.where(low, none, at_high)
                spread = jnp.concatenate(
                    [
                        jnp.concatenate(
                            [evens[:TOK], odds[TOK : 2 * TOK], none[:TOK]], axis=0
                        ),
                        jnp.concatenate([none[: 2 * TOK], evens[2 * TOK :]], axis=0),
                    ],
                    axis=1,
                )
                ordered = [p if i % 2 == head else swap_heads(p) for i, p in enumerate(prior)]
                stacked = jnp.concatenate(
                    [jnp.where(low[:TOK], ordered[0], ordered[1]), ordered[2]], axis=1
                )
                far = contract_lanes(fixed, evens if head == 0 else odds)
                near = contract_lanes(stacked, spread)
                top = jnp.maximum(
                    jnp.max(far, axis=0, keepdims=True), jnp.max(near, axis=0, keepdims=True)
                )
                far, near = jnp.exp(far - top), jnp.exp(near - top)
                total = jnp.sum(far, axis=0, keepdims=True)
                total += jnp.sum(near, axis=0, keepdims=True)
                inverse = 1.0 / total
                at = slice(pair * PAIR + head * HEAD_DIM, pair * PAIR + (head + 1) * HEAD_DIM)
                out_far = matmul(anchor_value[at, :], (far * inverse).astype(jnp.bfloat16))
                columns = [values[3 * group + f, at, :] for f in range(3)]
                out_near = matmul(
                    jnp.concatenate(columns, axis=0), (near * inverse).astype(jnp.bfloat16)
                )
                pick = out_near[:HEAD_DIM]
                for f in range(1, 3):
                    piece = out_near[f * HEAD_DIM : (f + 1) * HEAD_DIM]
                    pick = jnp.where(frame >= f * TOK, piece, pick)
                attended[group, at, :] = (out_far + pick).astype(jnp.bfloat16)
    copies[6].wait()
    copies[7].wait()
    for group in range(2):
        for base in range(0, part, PAIR):
            size = min(PAIR, part - base)
            mixed = matmul(transposed(attended[group, :, base : base + size]), w_out[...])
            at = slice(group * part + base, group * part + base + size)
            hid = (tok[at, :].astype(jnp.float32) + mixed).astype(jnp.bfloat16)
            hidden[at, :] = hid
            scaled = layer_norm(hid.astype(jnp.float32), conv_gain[...].reshape(1, C))
            active[at, :] = (scaled * (1.0 / (1.0 + jnp.exp(-scaled)))).astype(jnp.bfloat16)

    @pl.when(starts)
    def _():
        active[:TOK, :] = jnp.zeros((TOK, C), jnp.bfloat16)

    @pl.when(ends)
    def _():
        active[rows + TOK :, :] = jnp.zeros((TOK, C), jnp.bfloat16)

    results = ((hidden.at[TOK : rows + TOK, :], hidden_hbm), (active, active_hbm))
    for copy in fetch(results, out_sems):
        copy.wait()


def conv_kernel(
    own_hbm, y1, y2, y3, y4, partner_hbm, active_hbm, hidden_hbm, out_hbm,
    own, blocks, partner, active, hidden, weight, out, sems, out_sems,
):
    copies = fetch(
        (
            (own_hbm, own), (y1, blocks.at[0]), (y2, blocks.at[1]), (y3, blocks.at[2]),
            (y4, blocks.at[3]), (partner_hbm, partner), (active_hbm, active),
            (hidden_hbm, hidden),
        ),
        sems,
    )
    tm = lax.axis_index("tm")
    core = lax.rem(lax.axis_index("view"), 2)
    x, y = lax.rem(tm, X), lax.div(tm, X)
    sign = 1 - 2 * core

    def place(source, base, row):
        block = jnp.concatenate(
            [
                source[pl.ds(pl.multiple_of(base + (i ^ x) * SLOT, SLOT), SLOT), :][:SHARD]
                for i in range(X)
            ],
            axis=0,
        )
        weight[pl.ds(pl.multiple_of(row * (X * SHARD), 16), X * SHARD), :] = block

    copies[0].wait()
    place(own, 0, y)
    for s in range(4):
        copies[1 + s].wait()
        place(blocks.at[s], 0, (y - sign * (s + 1)) & (Y - 1))
    copies[5].wait()
    for s in range(3):
        place(partner, s * X * SLOT, (y + sign * (s + 1)) & (Y - 1))
    copies[6].wait()
    copies[7].wait()
    stores = []
    for f in range(out.shape[0] // TOK):
        at = slice(f * TOK, (f + 1) * TOK)
        mid = slice((f + 1) * TOK, (f + 2) * TOK)
        total = matmul(active[at, :], weight[:C, :])
        total += matmul(active[mid, :], weight[C : 2 * C, :])
        total += matmul(active[(f + 2) * TOK : (f + 3) * TOK, :], weight[2 * C :, :])
        out[at, :] = (hidden[at, :].astype(jnp.float32) + total).astype(jnp.bfloat16)
        stores += fetch(((out.at[at, :], out_hbm.at[at, :]),), (out_sems, f))
    for store in stores:
        store.wait()


def vmem(*shape):
    return pltpu.VMEM(shape, jnp.bfloat16)


def call(kernel, specs, outs, out_spec, scratch, flops, *operands):
    moved = sum(a.size * a.dtype.itemsize for a in operands)
    return pl.pallas_call(
        kernel,
        out_shape=[jax.ShapeDtypeStruct(s, jnp.bfloat16) for s in outs],
        in_specs=specs,
        out_specs=[out_spec] * len(outs),
        scratch_shapes=scratch,
        compiler_params=pltpu.CompilerParams(vmem_limit_bytes=LIMIT_BYTES),
        cost_estimate=pl.CostEstimate(flops=flops, bytes_accessed=moved, transcendentals=0),
    )(*operands)


def per_device(frames, ln_gain, w_query, w_key, w_value, w_out, conv_gain, conv_weight):
    local = frames.shape[1]
    rows = local * TOK
    tok = frames[0].reshape(rows, C)
    view, tm = lax.axis_index("view"), lax.axis_index("tm")
    x, y, z, core = tm % X, tm // X, view // 2, view % 2
    dma = pltpu.SemaphoreType.DMA
    wide = rows + 2 * TOK

    normed, q, last, first = call(
        query_kernel, [HBM] * 2 + [VMEM],
        [(rows, C), (rows, C), (2 * TOK, C), (TOK, C)], HBM,
        [vmem(rows, C), vmem(C, C), vmem(rows, C), vmem(rows, C), dma((2,)), dma((4,))],
        2 * rows * C * C,
        tok, w_query, ln_gain,
    )
    k, v = call(
        keys_kernel, [HBM] * 3, [(rows, C), (local, C, TOK)], HBM,
        [vmem(rows, C), vmem(C, C), vmem(C, C), vmem(rows, C), vmem(local, C, TOK),
         dma((3,)), dma((2,))],
        4 * rows * C * C,
        normed, w_key, w_value,
    )
    held, other, before, behind, blocks, partner = transfers(
        tok, last, first, conv_weight, (y, x, z), core
    )
    hidden, active = call(
        block_kernel, [VMEM] * 2 + [ANY] * 12, [(rows, C), (wide, C)], ANY,
        [vmem(C, C), vmem(C, C), vmem(C, C), vmem(C, C), vmem(wide, C), vmem(wide, C),
         vmem(wide, C), vmem(local + 2, C, TOK), vmem(TOK, C), vmem(C, TOK),
         vmem(2, TOK // 2, C), vmem(TOK, C), vmem(2, C, wide // 2), vmem(wide, C),
         vmem(wide, C), dma((13,)), dma((2,))],
        10 * rows * C * C,
        ln_gain, conv_gain, held, other, before, behind, w_key, w_value, w_query, q, k, v,
        tok, w_out,
    )
    (out,) = call(
        conv_kernel, [ANY] * 8, [(rows, C)], HBM,
        [vmem(X * SLOT, C), vmem(4, X * SLOT, C), vmem(3 * X * SLOT, C), vmem(wide, C),
         vmem(rows, C), vmem(3 * C, C), vmem(rows, C), dma((8,)), dma((local,))],
        6 * rows * C * C,
        *blocks, partner, active, hidden,
    )
    return out.reshape(1, local, TOK, C)


def solution(mesh):
    placed = (P("view", "tm", None, None), P(), P(), P(), P(), P(), P(), P("tm", None))

    return jax.shard_map(
        per_device,
        mesh=mesh,
        in_specs=placed,
        out_specs=P("view", "tm", None, None),
        check_vma=False,
    )
```

```python
import jax
import jax.numpy as jnp
from jax import lax
from jax.experimental import pallas as pl
from jax.experimental.pallas import tpu as pltpu
from jax.sharding import PartitionSpec as P


HEADS = 10
HEAD_DIM = 64
PAIR = 2 * HEAD_DIM
C = 640
TOK = 160
X, Y, Z = 4, 8, 8
TM = X * Y
AXES = ("view", "tm")
VMEM = pl.BlockSpec(memory_space=pltpu.VMEM)
SMEM = pl.BlockSpec(memory_space=pltpu.SMEM)
HBM = pl.BlockSpec(memory_space=pltpu.HBM)
ANY = pl.BlockSpec(memory_space=pl.ANY)
SHARD = 60
SLOT = 64
LIMIT_BYTES = 67043328


def device(y, x, z, core):
    return (z * 2 + core) * TM + y * X + x


def all_devices():
    return [
        (y, x, z, c) for z in range(Z) for c in range(2) for y in range(Y) for x in range(X)
    ]


def layer_norm(values, gain):
    mean = jnp.mean(values, axis=-1, keepdims=True)
    centred = values - mean
    variance = jnp.mean(centred * centred, axis=-1, keepdims=True)
    return centred * lax.rsqrt(variance + 1e-05) * gain


def matmul(a, b):
    return jnp.dot(a, b, preferred_element_type=jnp.float32)


ORDERS = (
    ((0, 4), (0, 2), (0, 1), (1, 2), (1, 1), (2, 4), (2, 2), (2, 1)),
    ((2, 4), (2, 2), (2, 1), (1, 2), (1, 1), (0, 4), (0, 2), (0, 1)),
)


def tree_pairs():
    holders = [[(0, 0, 0)], [(0, 0, 0)]]
    for step in range(8):
        pairs = []
        for core in range(2):
            dim, distance = ORDERS[core][step]
            fresh = []
            for place in holders[core]:
                target = list(place)
                target[dim] += distance
                fresh.append(tuple(target))
                pairs.append((device(*place, core), device(*target, core)))
            holders[core] = holders[core] + fresh
        yield pairs


def receives(step, place, core):
    flags = []
    for order in ORDERS:
        dim, distance = order[step]
        flag = place[dim] % (2 * distance) == distance
        seen = [d for d, _ in order[: step + 1]]
        for later in range(3):
            if later not in seen:
                flag = flag & (place[later] == 0)
        flags.append(flag)
    return jnp.where(core == 0, flags[0], flags[1])


def swapped_cores():
    return [(device(y, x, z, 1 - c), device(y, x, z, c)) for y, x, z, c in all_devices()]


def transfers(tok, last, first, shard, place, core):
    places = all_devices()
    half = TOK // 2
    second = tok[half:TOK]
    got = lax.ppermute(second, AXES, [(device(0, 0, 0, 0), device(0, 0, 0, 1))])
    top = lax.optimization_barrier(tok[:half])
    held = lax.select(jnp.broadcast_to(core == 0, got.shape), top, got)
    for step, pairs in enumerate(tree_pairs()):
        got = lax.ppermute(held, AXES, pairs)
        fresh = jnp.broadcast_to(receives(step, place, core), got.shape)
        held = lax.select(fresh, got, held)
    other = lax.ppermute(held, AXES, swapped_cores())
    behind = lax.ppermute(first, "tm", [(i + 1, i) for i in range(TM - 1)])
    before = lax.ppermute(last, "tm", [(i, i + 1) for i in range(TM - 1)])

    near = lax.ppermute(
        shard, AXES,
        [(device(y, x ^ 1, z, c), device(y, x, z, c)) for y, x, z, c in places],
    )
    slack = ((0, SLOT - SHARD), (0, 0))
    two = jnp.concatenate([jnp.pad(shard, slack), jnp.pad(near, slack)])
    far = lax.ppermute(
        two, AXES,
        [(device(y, x ^ 2, z, c), device(y, x, z, c)) for y, x, z, c in places],
    )
    own = jnp.concatenate([two, far])
    ring = [
        (device((y + (2 * c - 1)) % Y, x, z, c), device(y, x, z, c)) for y, x, z, c in places
    ]
    blocks = [own]
    for _ in range(4):
        blocks.append(lax.ppermute(blocks[-1], AXES, ring))
    partner = lax.ppermute(jnp.concatenate(blocks[1:4]), AXES, swapped_cores())
    return held, other, before, behind, blocks, partner


def transposed(values):
    return jnp.transpose(values.astype(jnp.float32)).astype(jnp.bfloat16)


def contract_lanes(a, b):
    return lax.dot_general(a, b, (((1,), (1,)), ((), ())), preferred_element_type=jnp.float32)


def swap_heads(a):
    return jnp.concatenate([a[:, HEAD_DIM:], a[:, :HEAD_DIM]], axis=1)


def fetch(pairs, sems):
    sems, start = sems if isinstance(sems, tuple) else (sems, 0)
    copies = [pltpu.make_async_copy(a, b, sems.at[start + i]) for i, (a, b) in enumerate(pairs)]
    for copy in copies:
        copy.start()
    return copies


def is_root():
    return (lax.axis_index("view") == 0) & (lax.axis_index("tm") == 0)


def normed_rows(raw, gain):
    part = layer_norm(raw.astype(jnp.float32), gain[...].reshape(1, C))
    return part.astype(jnp.bfloat16)


def query_kernel(
    tok_hbm, w_hbm, gain, normed_hbm, q_hbm, last_hbm, first_hbm, tok, w, normed, q, sems,
    out_sems,
):
    (load,) = fetch(((tok_hbm, tok),), sems)
    rows = tok.shape[0]
    load.wait()
    ends = fetch(
        ((tok.at[rows - 2 * TOK :, :], last_hbm), (tok.at[:TOK, :], first_hbm)), out_sems
    )

    @pl.when(jnp.logical_not(is_root()))
    def _():
        (load,) = fetch(((w_hbm, w),), (sems, 1))
        for at in range(0, rows, TOK):
            normed[at : at + TOK, :] = normed_rows(tok[at : at + TOK, :], gain)
        (first,) = fetch(((normed, normed_hbm),), (out_sems, 2))
        load.wait()
        q[...] = scaled_query(normed[...], w[...])
        (second,) = fetch(((q, q_hbm),), (out_sems, 3))
        first.wait()
        second.wait()

    for store in ends:
        store.wait()


def scaled_query(normed, w):
    part = matmul(normed, w).astype(jnp.bfloat16)
    return (part.astype(jnp.float32) * HEAD_DIM**-0.5).astype(jnp.bfloat16)


def keys_kernel(
    normed_hbm, w_k_hbm, w_v_hbm, k_hbm, v_hbm, normed, w_k, w_v, k, v, sems, out_sems
):
    @pl.when(jnp.logical_not(is_root()))
    def _():
        copies = fetch(((normed_hbm, normed), (w_k_hbm, w_k), (w_v_hbm, w_v)), sems)
        copies[0].wait()
        copies[1].wait()
        k[...] = matmul(normed[...], w_k[...]).astype(jnp.bfloat16)
        stores = fetch(((k, k_hbm),), out_sems)
        copies[2].wait()
        for f in range(v.shape[0]):
            v[f] = transposed(matmul(normed[f * TOK : (f + 1) * TOK, :], w_v[...]))
        stores += fetch(((v, v_hbm),), (out_sems, 1))
        for store in stores:
            store.wait()


def block_kernel(
    gain, conv_gain, held, other, before, behind, w_k_hbm, w_v_hbm, w_q_hbm, q_hbm, k_hbm,
    v_hbm, tok_hbm, w_out_hbm, hidden_hbm, active_hbm,
    w_k, w_v, w_q, w_out, tok, q, keys, values, anchor_key, anchor_value, halves, earlier,
    attended, hidden, active, sems, out_sems,
):
    count = tok_hbm.shape[0] // TOK
    rows, wide = count * TOK, (count + 2) * TOK
    tm = lax.axis_index("tm")
    core = lax.rem(lax.axis_index("view"), 2)
    starts, ends = tm == 0, tm == TM - 1

    @pl.when(starts)
    def _():
        pltpu.make_async_copy(tok_hbm.at[:TOK, :], tok.at[:TOK, :], sems.at[0]).start()

    @pl.when(jnp.logical_not(starts))
    def _():
        pltpu.make_async_copy(before.at[TOK:, :], tok.at[:TOK, :], sems.at[0]).start()

    inputs = fetch(
        (
            (held, halves.at[core]), (other, halves.at[1 - core]),
            (before.at[:TOK, :], earlier), (behind, tok.at[rows + TOK :, :]),
        ),
        (sems, 1),
    )
    copies = fetch(
        (
            (w_k_hbm, w_k), (w_v_hbm, w_v), (w_q_hbm, w_q), (q_hbm, q.at[TOK : rows + TOK, :]),
            (k_hbm, keys.at[2 * TOK :, :]), (v_hbm, values.at[2:]),
            (w_out_hbm, w_out), (tok_hbm, tok.at[TOK : rows + TOK, :]),
        ),
        (sems, 5),
    )
    pltpu.make_async_copy(before.at[TOK:, :], tok.at[:TOK, :], sems.at[0]).wait()
    for copy in inputs:
        copy.wait()

    anchor = normed_rows(jnp.concatenate([halves[0], halves[1]], axis=0), gain)
    second, first = normed_rows(earlier[...], gain), normed_rows(tok[:TOK, :], gain)
    final = normed_rows(tok[rows + TOK :, :], gain)
    copies[0].wait()
    anchor_key[...] = matmul(anchor, w_k[...]).astype(jnp.bfloat16)
    keys[:TOK, :] = matmul(second, w_k[...]).astype(jnp.bfloat16)
    keys[TOK : 2 * TOK, :] = matmul(first, w_k[...]).astype(jnp.bfloat16)
    copies[1].wait()
    anchor_value[...] = transposed(matmul(anchor, w_v[...]))
    values[0] = transposed(matmul(second, w_v[...]))
    values[1] = transposed(matmul(first, w_v[...]))
    copies[2].wait()
    q[:TOK, :] = scaled_query(first, w_q[...])
    q[rows + TOK :, :] = scaled_query(final, w_q[...])
    for copy in copies[3:6]:
        copy.wait()
    copies[7].wait()

    @pl.when(is_root())
    def _():
        for f in range(count):
            at = slice((f + 1) * TOK, (f + 2) * TOK)
            normed = normed_rows(tok[at, :], gain)
            q[at, :] = scaled_query(normed, w_q[...])
            keys[(f + 2) * TOK : (f + 3) * TOK, :] = matmul(normed, w_k[...]).astype(
                jnp.bfloat16
            )
            values[f + 2] = transposed(matmul(normed, w_v[...]))

    part = wide // 2
    frame = lax.broadcasted_iota(jnp.int32, (1, part), 1)
    low = lax.broadcasted_iota(jnp.int32, (part, PAIR), 1) < HEAD_DIM
    for group in range(2):
        at_q = slice(group * part, (group + 1) * part)
        for pair in range(HEADS // 2):
            lanes = slice(pair * PAIR, (pair + 1) * PAIR)
            query = q[at_q, lanes]
            turned = swap_heads(query)
            none = jnp.zeros_like(query)
            fixed = anchor_key[:, lanes]
            prior = [
                keys[group * part + f * TOK : group * part + (f + 1) * TOK, lanes]
                for f in range(3)
            ]
            for head in range(2):
                at_low, at_high = (query, turned) if head == 0 else (turned, query)
                evens = jnp.where(low, at_low, none)
                odds = jnp.where(low, none, at_high)
                spread = jnp.concatenate(
                    [
                        jnp.concatenate(
                            [evens[:TOK], odds[TOK : 2 * TOK], none[:TOK]], axis=0
                        ),
                        jnp.concatenate([none[: 2 * TOK], evens[2 * TOK :]], axis=0),
                    ],
                    axis=1,
                )
                ordered = [p if i % 2 == head else swap_heads(p) for i, p in enumerate(prior)]
                stacked = jnp.concatenate(
                    [jnp.where(low[:TOK], ordered[0], ordered[1]), ordered[2]], axis=1
                )
                far = contract_lanes(fixed, evens if head == 0 else odds)
                near = contract_lanes(stacked, spread)
                top = jnp.maximum(
                    jnp.max(far, axis=0, keepdims=True), jnp.max(near, axis=0, keepdims=True)
                )
                far, near = jnp.exp(far - top), jnp.exp(near - top)
                total = jnp.sum(far, axis=0, keepdims=True)
                total += jnp.sum(near, axis=0, keepdims=True)
                inverse = 1.0 / total
                at = slice(pair * PAIR + head * HEAD_DIM, pair * PAIR + (head + 1) * HEAD_DIM)
                out_far = matmul(anchor_value[at, :], (far * inverse).astype(jnp.bfloat16))
                columns = [values[3 * group + f, at, :] for f in range(3)]
                out_near = matmul(
                    jnp.concatenate(columns, axis=0), (near * inverse).astype(jnp.bfloat16)
                )
                pick = out_near[:HEAD_DIM]
                for f in range(1, 3):
                    piece = out_near[f * HEAD_DIM : (f + 1) * HEAD_DIM]
                    pick = jnp.where(frame >= f * TOK, piece, pick)
                attended[group, at, :] = (out_far + pick).astype(jnp.bfloat16)
    copies[6].wait()
    for group in range(2):
        for base in range(0, part, PAIR):
            size = min(PAIR, part - base)
            mixed = matmul(transposed(attended[group, :, base : base + size]), w_out[...])
            at = slice(group * part + base, group * part + base + size)
            hid = (tok[at, :].astype(jnp.float32) + mixed).astype(jnp.bfloat16)
            hidden[at, :] = hid
            scaled = layer_norm(hid.astype(jnp.float32), conv_gain[...].reshape(1, C))
            active[at, :] = (scaled * (1.0 / (1.0 + jnp.exp(-scaled)))).astype(jnp.bfloat16)

    @pl.when(starts)
    def _():
        active[:TOK, :] = jnp.zeros((TOK, C), jnp.bfloat16)

    @pl.when(ends)
    def _():
        active[rows + TOK :, :] = jnp.zeros((TOK, C), jnp.bfloat16)

    results = ((hidden.at[TOK : rows + TOK, :], hidden_hbm), (active, active_hbm))
    for copy in fetch(results, out_sems):
        copy.wait()


def conv_kernel(
    own_hbm, y1, y2, y3, y4, partner_hbm, active_hbm, hidden_hbm, out_hbm,
    own, blocks, partner, active, hidden, weight, out, sems, out_sems,
):
    copies = fetch(
        (
            (own_hbm, own), (y1, blocks.at[0]), (y2, blocks.at[1]), (y3, blocks.at[2]),
            (y4, blocks.at[3]), (partner_hbm, partner), (active_hbm, active),
            (hidden_hbm, hidden),
        ),
        sems,
    )
    tm = lax.axis_index("tm")
    core = lax.rem(lax.axis_index("view"), 2)
    x, y = lax.rem(tm, X), lax.div(tm, X)
    sign = 1 - 2 * core

    def place(source, base, row):
        block = jnp.concatenate(
            [
                source[pl.ds(pl.multiple_of(base + (i ^ x) * SLOT, SLOT), SLOT), :][:SHARD]
                for i in range(X)
            ],
            axis=0,
        )
        weight[pl.ds(pl.multiple_of(row * (X * SHARD), 16), X * SHARD), :] = block

    copies[0].wait()
    place(own, 0, y)
    for s in range(4):
        copies[1 + s].wait()
        place(blocks.at[s], 0, (y - sign * (s + 1)) & (Y - 1))
    copies[5].wait()
    for s in range(3):
        place(partner, s * X * SLOT, (y + sign * (s + 1)) & (Y - 1))
    copies[6].wait()
    copies[7].wait()
    stores = []
    for f in range(out.shape[0] // TOK):
        at = slice(f * TOK, (f + 1) * TOK)
        mid = slice((f + 1) * TOK, (f + 2) * TOK)
        total = matmul(active[at, :], weight[:C, :])
        total += matmul(active[mid, :], weight[C : 2 * C, :])
        total += matmul(active[(f + 2) * TOK : (f + 3) * TOK, :], weight[2 * C :, :])
        out[at, :] = (hidden[at, :].astype(jnp.float32) + total).astype(jnp.bfloat16)
        stores += fetch(((out.at[at, :], out_hbm.at[at, :]),), (out_sems, f))
    for store in stores:
        store.wait()


def vmem(*shape):
    return pltpu.VMEM(shape, jnp.bfloat16)


def call(kernel, specs, outs, out_spec, scratch, flops, *operands):
    moved = sum(a.size * a.dtype.itemsize for a in operands)
    return pl.pallas_call(
        kernel,
        out_shape=[jax.ShapeDtypeStruct(s, jnp.bfloat16) for s in outs],
        in_specs=specs,
        out_specs=[out_spec] * len(outs),
        scratch_shapes=scratch,
        compiler_params=pltpu.CompilerParams(vmem_limit_bytes=LIMIT_BYTES),
        cost_estimate=pl.CostEstimate(flops=flops, bytes_accessed=moved, transcendentals=0),
    )(*operands)


def per_device(frames, ln_gain, w_query, w_key, w_value, w_out, conv_gain, conv_weight):
    local = frames.shape[1]
    rows = local * TOK
    tok = frames[0].reshape(rows, C)
    view, tm = lax.axis_index("view"), lax.axis_index("tm")
    x, y, z, core = tm % X, tm // X, view // 2, view % 2
    dma = pltpu.SemaphoreType.DMA
    wide = rows + 2 * TOK

    normed, q, last, first = call(
        query_kernel, [HBM] * 2 + [VMEM],
        [(rows, C), (rows, C), (2 * TOK, C), (TOK, C)], HBM,
        [vmem(rows, C), vmem(C, C), vmem(rows, C), vmem(rows, C), dma((2,)), dma((4,))],
        2 * rows * C * C,
        tok, w_query, ln_gain,
    )
    k, v = call(
        keys_kernel, [HBM] * 3, [(rows, C), (local, C, TOK)], HBM,
        [vmem(rows, C), vmem(C, C), vmem(C, C), vmem(rows, C), vmem(local, C, TOK),
         dma((3,)), dma((2,))],
        4 * rows * C * C,
        normed, w_key, w_value,
    )
    held, other, before, behind, blocks, partner = transfers(
        tok, last, first, conv_weight, (y, x, z), core
    )
    hidden, active = call(
        block_kernel, [VMEM] * 2 + [ANY] * 12, [(rows, C), (wide, C)], ANY,
        [vmem(C, C), vmem(C, C), vmem(C, C), vmem(C, C), vmem(wide, C), vmem(wide, C),
         vmem(wide, C), vmem(local + 2, C, TOK), vmem(TOK, C), vmem(C, TOK),
         vmem(2, TOK // 2, C), vmem(TOK, C), vmem(2, C, wide // 2), vmem(wide, C),
         vmem(wide, C), dma((13,)), dma((2,))],
        10 * rows * C * C,
        ln_gain, conv_gain, held, other, before, behind, w_key, w_value, w_query, q, k, v,
        tok, w_out,
    )
    (out,) = call(
        conv_kernel, [ANY] * 8, [(rows, C)], HBM,
        [vmem(X * SLOT, C), vmem(4, X * SLOT, C), vmem(3 * X * SLOT, C), vmem(wide, C),
         vmem(rows, C), vmem(3 * C, C), vmem(rows, C), dma((8,)), dma((local,))],
        6 * rows * C * C,
        *blocks, partner, active, hidden,
    )
    return out.reshape(1, local, TOK, C)


def solution(mesh):
    placed = (P("view", "tm", None, None), P(), P(), P(), P(), P(), P(), P("tm", None))

    return jax.shard_map(
        per_device,
        mesh=mesh,
        in_specs=placed,
        out_specs=P("view", "tm", None, None),
        check_vma=False,
    )
```
